32 devices in a mesh: tok: 4 (over z), lat: 4 (over y, x), src: 2 (over core).
Axes of the slice: x: 2, y: 2, z: 4, core: 2. Of those that a mesh axis runs over, the one named last changes fastest.
Arguments:
- residuals: bfloat16 [2, 1024, 8192], P('src', 'tok', 'lat'), may hold values from -6 to 6
- enc_weight: bfloat16 [2, 8192, 8192], P('src', 'tok', 'lat'), may hold values from -0.046875 to 0.046875
- dec_weight: bfloat16 [2, 8192, 8192], P('src', 'lat', 'tok'), may hold values from -0.09375 to 0.09375
- enc_bias: float32 [8192], P('lat'), may hold values from -3 to 3
- dec_bias: float32 [2, 8192], P('src', 'tok'), may hold values from -3 to 3
- active: int32 [1024, 8192], P('tok', 'lat'), may hold values 0 or 1
Outputs:
- latent_codes: bfloat16 [1024, 8192], P('tok', 'lat')
- rebuilt: bfloat16 [2, 1024, 8192], P('src', 'lat', 'tok')
The draws below stay inside these ranges and needn't reach their ends.
Inputs may be any that keep to these rules, and one draw needn't show every extreme that they name: `active`: each entry is 0 or 1. The number of kept latents of a token, or of a device's block, has no bound below the full shape that may be relied on.
All inputs are finite; a program needn't handle non-finite values.
Results may differ from the reference program's by a relative error of at most 0.0045.
Values may be sent and summed in bfloat16 or wider, within the bound.
No kernel may reach another device: no remote copies, remote signals or barrier semaphores. Data moves between devices by JAX's collectives and lax.ppermute only.
A program may use at most 128 MiB of HBM per device.

```python
import jax
import jax.numpy as jnp

D = 8192
LATENTS = 8192
TOKENS = 1024


def plant(array, stream_key, low, largest):
    longest = array.shape.index(max(array.shape))
    spots = []
    for shift in (0, 1):
        where = [jax.random.randint(jax.random.fold_in(stream_key, axis), (), 0, length) for axis, length in enumerate(array.shape)]
        where[longest] = (where[longest] + shift) % array.shape[longest]
        spots.append(tuple(where))
    return array.at[spots[0]].set(low).at[spots[1]].set(largest)


def levels(key, shape, split, least, high):
    factor_of, own = 1.0, jax.random.fold_in(key, 6)
    for position, parts in split:
        steps = jnp.exp(jax.random.uniform(jax.random.fold_in(own, position), (parts,), jnp.float32, least / len(split), high / len(split)))
        factor_of = factor_of * jnp.repeat(steps, shape[position] // parts).reshape([-1 if axis == position else 1 for axis in range(len(shape))])
    return factor_of


def centred(key, shape, width, bound, shards=(), dtype=jnp.bfloat16):
    drawn = width * jax.random.normal(key, shape, jnp.float32)
    if shards:
        drawn = drawn * levels(key, shape, shards, -0.22, 0.18)
    return jnp.clip(drawn, -bound, bound).astype(dtype)


def setup_inputs(seed: int = 0) -> dict:
    seeds = jax.random.split(jax.random.key(seed), 7)
    residuals = centred(seeds[0], (2, TOKENS, D), 1.0, 6.0, ((0, 2), (1, 4), (2, 4)))
    enc_weight = centred(seeds[1], (2, D, LATENTS), (2 * D) ** -0.5, 0.046875, ((0, 2), (1, 4), (2, 4)))
    dec_weight = centred(seeds[2], (2, LATENTS, D), (LATENTS // 2) ** -0.5, 0.09375, ((0, 2), (1, 4), (2, 4)))
    enc_bias = centred(seeds[3], (LATENTS,), 0.5, 3.0, ((0, 4),), jnp.float32)
    dec_bias = centred(seeds[4], (2, D), 0.5, 3.0, ((0, 2), (1, 4)), jnp.float32)
    active = plant((jax.random.randint(seeds[5], (TOKENS, LATENTS), 0, 4) < 3).astype(jnp.int32), jax.random.fold_in(seeds[5], 1), 0, 1)
    return dict(residuals=residuals, enc_weight=enc_weight, dec_weight=dec_weight, enc_bias=enc_bias, dec_bias=dec_bias, active=active)


def reference(residuals, enc_weight, dec_weight, enc_bias, dec_bias, active):
    preact = jnp.dot(residuals[0], enc_weight[0], preferred_element_type=jnp.float32)
    preact = preact + jnp.dot(residuals[1], enc_weight[1], preferred_element_type=jnp.float32)
    preact = preact + enc_bias[None, :]
    positive = jnp.maximum(preact, 0.0)
    latent_codes = jnp.where(active == 1, positive, 0.0).astype(jnp.bfloat16)
    first = jnp.dot(latent_codes, dec_weight[0], preferred_element_type=jnp.float32) + dec_bias[0][None, :]
    second = jnp.dot(latent_codes, dec_weight[1], preferred_element_type=jnp.float32) + dec_bias[1][None, :]
    rebuilt = jnp.stack([first, second]).astype(jnp.bfloat16)
    return latent_codes, rebuilt
```

```python
import functools

import jax
import jax.numpy as jnp
from jax import lax
from jax.experimental import pallas as pl
from jax.experimental.pallas import tpu as pltpu
from jax.sharding import PartitionSpec as P

CHUNKS = 2
BF16, F32 = jnp.bfloat16, jnp.float32


def swap(x, axis, n, k):
    return lax.ppermute(x, axis, [(i, i ^ k) for i in range(n)])


def tile_of(width):
    return min(512, width)


def encoder_kernel(n, masks, place_ref, *refs):
    pieces, (weight, keep, send, held) = refs[:-4], refs[-4:]
    pairs, half = len(masks), held.shape[3]

    @pl.when(pl.program_id(0) == 0)
    def _():
        base, core = place_ref[0] >> 1, place_ref[0] & 1
        for i, mask in enumerate(masks):
            for k in range(n):
                block = base ^ (k ^ mask)
                rows = pieces[i * n + k]
                held[core, block, i] = rows[:half]
                held[1 - core, block, i] = rows[half:]

    count = n * pairs * half
    left = held[...].reshape(2 * count, held.shape[4])
    out = jnp.dot(left, weight[...], preferred_element_type=F32)
    keep[...] = out[:count].reshape(keep.shape)
    send[...] = out[count:].astype(BF16).reshape(send.shape)


def encode(n, masks, place, pieces, weight):
    depth, width = weight.shape
    half, pairs, tile = pieces[0].shape[0] // 2, len(masks), tile_of(width)
    whole = pl.BlockSpec(pieces[0].shape, lambda i, p: (0, 0))
    out = pl.BlockSpec((n, pairs * half, tile), lambda i, p: (0, 0, i))
    shape = (n, pairs * half, width)
    rows = 2 * n * pairs * half
    return pl.pallas_call(
        functools.partial(encoder_kernel, n, masks),
        grid_spec=pltpu.PrefetchScalarGridSpec(
            num_scalar_prefetch=1,
            grid=(width // tile,),
            in_specs=[whole] * len(pieces) + [pl.BlockSpec((depth, tile), lambda i, p: (0, i))],
            out_specs=[out, out],
            scratch_shapes=[pltpu.VMEM((2, n, pairs, half, depth), BF16)],
        ),
        out_shape=[jax.ShapeDtypeStruct(shape, F32), jax.ShapeDtypeStruct(shape, BF16)],
        cost_estimate=pl.CostEstimate(
            flops=2 * rows * depth * width,
            bytes_accessed=2 * depth * width + 2 * rows * depth + 3 * rows * width,
            transcendentals=0,
        ),
        name="encoder",
    )(place, *pieces, weight)


def decoder_kernel(n, pairs, place_ref, *refs):
    pieces, weight = refs[: 2 * n], refs[2 * n]
    own, keep, sends, held = refs[2 * n + 1], refs[2 * n + 2], refs[2 * n + 3 : -1], refs[-1]
    half = held.shape[3]

    @pl.when(pl.program_id(0) == 0)
    def _():
        base, core = place_ref[0] >> 1, place_ref[0] & 1
        for q in range(n):
            for i in range(pairs):
                rows = pl.ds(i * half, half)
                held[base ^ q, i, core] = pieces[q][rows]
                held[base ^ q, i, 1 - core] = pieces[n + q][rows]
        own[...] = held[base].reshape(own.shape)

    count = pairs * 2 * half
    left = held[...].reshape(n * count, held.shape[4])
    out = jnp.dot(left, weight[...], preferred_element_type=F32)
    keep[...] = out[:count]
    for m in range(1, n):
        sends[m - 1][...] = out[m * count : (m + 1) * count].astype(BF16)


def decode(n, pairs, place, pieces, weight):
    depth, width = weight.shape
    half, tile = pieces[0].shape[0] // pairs, tile_of(width)
    count = pairs * 2 * half
    whole = pl.BlockSpec(pieces[0].shape, lambda i, p: (0, 0))
    out = pl.BlockSpec((count, tile), lambda i, p: (0, i))
    sent = jax.ShapeDtypeStruct((count, width), BF16)
    rows = n * count
    return pl.pallas_call(
        functools.partial(decoder_kernel, n, pairs),
        grid_spec=pltpu.PrefetchScalarGridSpec(
            num_scalar_prefetch=1,
            grid=(width // tile,),
            in_specs=[whole] * len(pieces) + [pl.BlockSpec((depth, tile), lambda i, p: (0, i))],
            out_specs=[pl.BlockSpec((count, depth), lambda i, p: (0, 0))] + [out] * n,
            scratch_shapes=[pltpu.VMEM((n, pairs, 2, half, depth), BF16)],
        ),
        out_shape=[jax.ShapeDtypeStruct((count, depth), BF16), jax.ShapeDtypeStruct((count, width), F32)] + [sent] * (n - 1),
        cost_estimate=pl.CostEstimate(
            flops=2 * rows * depth * width,
            bytes_accessed=2 * depth * width + 4 * rows * depth + 3 * rows * width,
            transcendentals=0,
        ),
        name="decoder",
    )(place, *pieces, weight)


def per_device(n, cores, residuals, enc_weight, dec_weight, enc_bias, dec_bias, active):
    rows, encoder, decoder = residuals[0], enc_weight[0], dec_weight[0]
    tok, lat, core = lax.axis_index("tok"), lax.axis_index("lat"), lax.axis_index("src")
    place = (((tok ^ lat) << 1) | core).astype(jnp.int32).reshape(1)
    piece = rows.shape[0] // n
    half, pairs = piece // 2, n // CHUNKS
    order = sorted(range(n), key=lambda m: (bin(m).count("1") & 1, m))
    masks = [order[c * pairs : (c + 1) * pairs] for c in range(CHUNKS)]
    arrived = []
    for i, mask in enumerate(order):
        ring = [(t * n + l, l * n + (t ^ mask)) for t in range(n) for l in range(n)]
        arrived.append(lax.ppermute(rows[i * piece : (i + 1) * piece], ("tok", "lat"), ring))
    chosen = active.reshape(n, 2, half, active.shape[1])
    chosen = lax.dynamic_index_in_dim(chosen, core, 1, keepdims=False)

    codes_out, rebuilt_out = [], []
    for c in range(CHUNKS):
        pieces = []
        for i in range(pairs):
            mine = arrived[c * pairs + i]
            pieces += [mine] + [swap(mine, "lat", n, k) for k in range(1, n)]
        keep, send = encode(n, masks[c], place, pieces, encoder)
        total = keep + lax.ppermute(send, "src", [(0, 1), (1, 0)])
        pre = total[0]
        for q in range(1, n):
            pre = pre + swap(total[q].astype(BF16), "tok", n, q)
        positive = jnp.maximum(pre + enc_bias[None, :], 0.0)
        on = chosen[c * pairs : (c + 1) * pairs].reshape(pairs * half, -1)
        codes = jnp.where(on == 1, positive, 0.0).astype(BF16)
        mine = [codes] + [swap(codes, "tok", n, q) for q in range(1, n)]
        other = [lax.ppermute(x, "src", [(0, 1), (1, 0)]) for x in mine]
        own, keep, *sends = decode(n, pairs, place, mine + other, decoder)
        for m in range(1, n):
            keep = keep + swap(sends[m - 1], "lat", n, m)
        codes_out.append(own)
        rebuilt_out.append((keep + dec_bias[0][None, :]).astype(BF16))
    return jnp.concatenate(codes_out), jnp.concatenate(rebuilt_out)[None]


def solution(mesh):
    n, cores = mesh.shape["tok"], mesh.shape["src"]
    assert n == mesh.shape["lat"] and cores == 2
    return jax.shard_map(
        functools.partial(per_device, n, cores),
        mesh=mesh,
        in_specs=(
            P("src", "tok", "lat"),
            P("src", "tok", "lat"),
            P("src", "lat", "tok"),
            P("lat"),
            P("src", "tok"),
            P("tok", "lat"),
        ),
        out_specs=(P("tok", "lat"), P("src", "lat", "tok")),
        check_vma=False,
    )
```
